256 devices in a mesh: seq: 64 (over z, y, core), tp: 4 (over x).
Axes of the slice: x: 4, y: 4, z: 8, core: 2. Of those that a mesh axis runs over, the one named last changes fastest.
Arguments:
- tokens: bfloat16 [8192, 3584], P('seq', 'tp'), may hold values from -24 to 24
- modality: int32 [64], P('seq'), may hold values from 0 to 1
- segment: int32 [8192], P('seq'), may hold values from 0 to 3, never falling along the last dimension, each value on 1 to 4096 neighbouring positions
- w_proj: bfloat16 [2, 3584, 4608], P(None, 'seq', 'tp'), may hold values from -1 to 1
Outputs:
- attended: bfloat16 [8192, 3584], P('seq', 'tp')
The draws below stay inside these ranges and needn't reach their ends.
Inputs may be any that keep to these rules, and one draw needn't show every extreme that they name: `modality`: 128 consecutive tokens share one label: 0 marks an understanding block, 1 a generation block. `segment`: sample numbers never fall along the tokens.
All inputs are finite; a program needn't handle non-finite values.
Results may differ from the reference program's by a relative error of at most 0.0086.
Values may be sent and summed in bfloat16 or wider, within the bound.
A program may use at most 128 MiB of HBM per device.

```python
import math
import jax
import jax.numpy as jnp
import numpy as np
from jax import lax

MODEL_WIDTH = 3584
QUERY_HEADS = 28
KEY_VALUE_HEADS = 4
HEAD_SIZE = 128
MODALITY_BLOCK = 128
TOKENS = 8192
QKV = 4608


def draw_tokens(key, part):
    drawn_draw = jax.random.truncated_normal(key, -6.0, 6.0, (TOKENS, MODEL_WIDTH), jnp.float32)
    return drawn_draw.astype(jnp.bfloat16)


def draw_w_proj(key, part):
    group_width = QUERY_HEADS // KEY_VALUE_HEADS
    random_noise_key = jax.random.fold_in(jax.random.fold_in(key, 202), 0)
    noise_sample_draw = jax.random.truncated_normal(random_noise_key, -6.0, 6.0, (2, MODEL_WIDTH, KEY_VALUE_HEADS, group_width + 2, HEAD_SIZE), jnp.float32)
    query_scale = math.sqrt(2.0 / MODEL_WIDTH)
    value_scale = 2.0 / math.sqrt(MODEL_WIDTH)
    query_key = noise_sample_draw[:, :, :, :group_width + 1] * query_scale
    value_cols = noise_sample_draw[:, :, :, group_width + 1:] * value_scale
    joined = jnp.concatenate([query_key, value_cols], axis=3)
    return jnp.clip(joined, -1.0, 1.0).reshape(2, MODEL_WIDTH, QKV).astype(jnp.bfloat16)


def place_ends(values, key, low, largest):
    shape = values.shape
    index_at = [jax.random.randint(jax.random.fold_in(key, axis), (), 0, shape[axis]) for axis in range(len(shape))]
    values = values.at[tuple(index_at)].set(low)
    longest = shape.index(max(shape))
    index_at[longest] = (index_at[longest] + 1) % shape[longest]
    return values.at[tuple(index_at)].set(largest)


def profile(count, total, limit, lean):
    loads = [(1 << 20) // math.isqrt(grade ** lean) + 1 for grade in range(2, count + 1)]
    surplus, given = total - limit - (count - 1), [1] * (count - 1)
    while surplus > 0:
        candidates = [i for i in range(count - 1) if given[i] < limit]
        pool, left = sum([loads[i] for i in candidates]), surplus
        for i in candidates:
            more = min(limit - given[i], max(1, left * loads[i] // pool), surplus)
            given[i] = given[i] + more
            surplus = surplus - more
    return np.array([limit] + given)


def uneven(key, amount, total, bound, lean):
    if amount == 2:
        one = jax.random.randint(key, (), max(1, total - bound), min(bound, total - 1) + 1)
        return jnp.stack([one, total - one])
    tallies = jnp.asarray(profile(amount, total, bound, lean), jnp.int32)
    twos = (amount - 1) // 2
    source_of, sink = tallies[1:1 + 2 * twos:2], tallies[2:2 + 2 * twos:2]
    slack = jnp.minimum(source_of - 1, bound - sink)
    shifted = jax.random.randint(jax.random.fold_in(key, 1), (twos,), 0, 1 << 20) % (slack + 1)
    tallies = tallies.at[1:1 + 2 * twos:2].set(source_of - shifted).at[2:2 + 2 * twos:2].set(sink + shifted)
    return tallies[jax.random.permutation(jax.random.fold_in(key, 2), amount)]


def setup_inputs(seed: int = 0) -> dict:
    seeds = jax.random.split(jax.random.key(seed), 5)
    return {
        "tokens": draw_tokens(jax.random.fold_in(seeds[4], 71), 0),
        "modality": place_ends(jax.random.randint(seeds[1], (TOKENS // MODALITY_BLOCK,), 0, 2), jax.random.fold_in(seeds[1], 1), 0, 1).astype(jnp.int32),
        "segment": jnp.searchsorted(jnp.cumsum(uneven(seeds[2], 4, TOKENS, TOKENS // 2, 0)), jnp.arange(TOKENS), side="right").astype(jnp.int32),
        "w_proj": draw_w_proj(jax.random.fold_in(seeds[4], 71), 0),
    }


masked_score = -1e+30

def reference(tokens, modality, segment, w_proj):
    head_groups = QUERY_HEADS // KEY_VALUE_HEADS
    total_token_count = tokens.shape[0]
    label_rows = jnp.repeat(modality, MODALITY_BLOCK)
    under_proj = jnp.dot(tokens, w_proj[0], preferred_element_type=jnp.float32)
    gen_proj = jnp.dot(tokens, w_proj[1], preferred_element_type=jnp.float32)
    projected_tokens = jnp.where(label_rows[:, None] == 1, gen_proj, under_proj).astype(jnp.bfloat16)
    projected_tokens = lax.optimization_barrier(projected_tokens).astype(jnp.float32)
    projected_tokens = projected_tokens.reshape(total_token_count, KEY_VALUE_HEADS, head_groups + 2, HEAD_SIZE)
    queries = projected_tokens[:, :, :head_groups]
    key_rows = projected_tokens[:, :, head_groups]
    values = projected_tokens[:, :, head_groups + 1]
    positions = jnp.arange(total_token_count, dtype=jnp.int32)

    def one_block(block_index):
        offset = block_index * MODALITY_BLOCK
        query_rows = lax.dynamic_slice_in_dim(queries, offset, MODALITY_BLOCK, 0)
        query_pos = offset + jnp.arange(MODALITY_BLOCK, dtype=jnp.int32)
        query_seg = lax.dynamic_slice_in_dim(segment, offset, MODALITY_BLOCK, 0)
        query_gen = lax.dynamic_index_in_dim(modality, block_index, 0, keepdims=False) == 1
        allowed = (query_seg[:, None] == segment[None, :]) & ((positions[None, :] <= query_pos[:, None]) | (positions[None, :] // MODALITY_BLOCK == block_index) & query_gen)
        scores = jnp.einsum('qgrd,kgd->grqk', query_rows, key_rows, precision=lax.Precision.HIGHEST) / math.sqrt(HEAD_SIZE)
        scores = jnp.where(allowed[None, None], scores, masked_score)
        row_max = lax.optimization_barrier(jnp.max(scores, axis=3, keepdims=True))
        weights = jnp.where(allowed[None, None], jnp.exp(scores - row_max), 0.0)
        weight_sum = lax.optimization_barrier(jnp.sum(weights, axis=3))
        rounded = lax.optimization_barrier(weights.astype(jnp.bfloat16)).astype(jnp.float32)
        numerator = jnp.einsum('grqk,kgd->qgrd', rounded, values, precision=lax.Precision.HIGHEST)
        attended = numerator / jnp.transpose(weight_sum, (2, 0, 1))[:, :, :, None]
        return attended.astype(jnp.bfloat16).reshape(MODALITY_BLOCK, KEY_VALUE_HEADS * head_groups * HEAD_SIZE)
    attended = lax.map(one_block, jnp.arange(total_token_count // MODALITY_BLOCK, dtype=jnp.int32))
    return attended.reshape(total_token_count, QUERY_HEADS * HEAD_SIZE)
```

```python
import math

import jax
import jax.numpy as jnp
from jax import lax
from jax.experimental import pallas as pl
from jax.experimental.pallas import tpu as pltpu
from jax.sharding import PartitionSpec as P

HEADS = 7
D = 128
BLOCK = 128
WINDOW = 33
CHUNKS = 3
PER = WINDOW // CHUNKS
FAR = -1e30
SCALE = math.log2(math.e) / math.sqrt(D)
MESH = pl.DeviceIdType.MESH
DEPTH = 3584
PART = DEPTH // 4
SLAB = 56
PLANE = 8 * SLAB
ROWS = 144
COPIES = 200


def project(tok, w, meta, proj, kv, T, W, mb, acc, ob, vb, vp, send, recv, near):
    s, x = lax.axis_index("seq"), lax.axis_index("tp")
    z, y, c = s // 8, (s // 2) % 4, s % 2

    def at(dz=0, dy=0, dc=0, dx=0):
        return (((z + dz) % 8) * 8 + ((y + dy) % 4) * 2 + (c + dc) % 2, (x + dx) % 4)

    made = []

    def remote(src, dst, device):
        k = len(made)
        made.append(
            pltpu.make_async_remote_copy(
                src_ref=src,
                dst_ref=dst,
                send_sem=send.at[k],
                recv_sem=recv.at[k],
                device_id=device,
                device_id_type=MESH,
            )
        )
        return made[-1]

    def go(src, dst, device):
        copy = remote(src, dst, device)
        copy.start()
        return copy

    barrier = pltpu.get_barrier_semaphore()
    peers = [at(dx=1), at(dx=3), at(dz=1), at(dz=7)]
    peers += [at(dy=d, dc=e) for d in range(4) for e in range(2) if d or e]
    for peer in peers:
        pl.semaphore_signal(barrier, inc=1, device_id=peer, device_id_type=MESH)
    pl.semaphore_wait(barrier, len(peers))

    def cols(j):
        return pl.ds(pl.multiple_of((j % 4) * PART, 128), PART)

    def rows_of(plane):
        return pl.ds(pl.multiple_of(((plane + 8) % 8) * PLANE, 64), PLANE)

    def head_cols(j):
        return pl.ds(pl.multiple_of(j * D, 128), D)

    mine = pl.ds(pl.multiple_of(s * SLAB, 8), SLAB)
    spread = z // 2

    local = []
    first, ninth = [], []
    for d in range(4):
        for e in range(2):
            there, m = (y + d) % 4, (c + e) % 2
            for h in range(2):
                src, dst = w.at[m, :, head_cols(2 * there + h)], W.at[m, h, mine, :]
                if d or e:
                    first.append(go(src, dst, at(dy=d, dc=e)))
                else:
                    local.append(pltpu.make_async_copy(src, dst, near.at[h]))
                    local[-1].start()
            src, dst = w.at[m, :, pl.ds(8 * D, D)], W.at[m, 2, mine, :]
            if d or e:
                copy = remote(src, dst, at(dy=d, dc=e))
                ninth.append((d, copy))
                pl.when(there == spread)(copy.start)
            else:
                own = pltpu.make_async_copy(src, dst, near.at[2])
                pl.when(y == spread)(own.start)
    metas = [
        go(meta, mb.at[y * 2 + c], at(dy=d, dc=e)) for d in range(4) for e in range(2) if d or e
    ]
    for src, dst, k in (
        (tok, T.at[y, :, cols(x)], 3),
        (meta, mb.at[y * 2 + c], 4),
    ):
        local.append(pltpu.make_async_copy(src, dst, near.at[k]))
        local[-1].start()

    class Ring:
        def __init__(self, axis, piece, src=None):
            self.axis, self.piece = axis, piece
            self.me = y if axis == "dy" else x
            own = piece(self.me % 4, None) if src is None else src
            self.a = go(own, piece(self.me % 4, None), at(**{axis: 1}))
            self.b = go(own, piece(self.me % 4, None), at(**{axis: 3}))

        def forward(self):
            self.a.wait_recv()
            part = self.piece((self.me + 3) % 4, 0)
            self.f = go(part, part, at(**{self.axis: 1}))
            self.b.wait_recv()
            part = self.piece((self.me + 1) % 4, 1)
            self.g = go(part, part, at(**{self.axis: 3}))

        def finish(self):
            self.f.wait_recv()
            self.g.wait_recv()

    def top_piece(row, j, half):
        r = pl.ds(0, 64) if half is None else pl.ds(32 * half, 32)
        return T.at[row % 4, r, cols(j)]

    def low_piece(row, j, half):
        r = pl.ds(64, 64) if half is None else pl.ds(64 + 32 * half, 32)
        return T.at[row % 4, r, cols(j)]

    top, low = tok.at[pl.ds(0, 64), :], tok.at[pl.ds(64, 64), :]
    top_y = Ring("dy", lambda j, h: top_piece(j, x, h), top)
    low_x = Ring("dx", lambda j, h: low_piece(y, j, h), low)
    top_x = [Ring("dx", lambda j, h: top_piece(y, j, h), top)]
    low_y = [Ring("dy", lambda j, h: low_piece(j, x, h), low)]

    def top_more(d):
        top_x.append(Ring("dx", lambda j, h: top_piece(y + d, j, h)))

    def low_more(d):
        low_y.append(Ring("dy", lambda j, h: low_piece(j, x + d, h)))

    for copy in first:
        copy.wait_recv()
    for copy in local[:2]:
        copy.wait()

    @pl.when(y == spread)
    def _():
        for _, copy in ninth:
            copy.wait_recv()
        own.wait()

    def third(o):
        return ((o + 8) % 8) // 2 == y

    ring, side, special, special_side = {}, [], {}, []

    def share(h, o, rows=None):
        ref = W.at[c, h, rows_of(o) if rows is None else rows, :]
        side.append(go(ref, ref, at(dc=1)))

    def half_rows(o, half):
        return pl.ds(pl.multiple_of(((o + 8) % 8) * PLANE + half * (PLANE // 2), 32), PLANE // 2)

    def launch(t):
        for way, sign in ((0, 1), (1, -1)):
            o = z - sign * t
            for h in range(2) if t < 3 else (way,):
                ref = W.at[c, h, rows_of(o), :]
                ring[way, t, h] = go(ref, ref, at(dz=1 if way == 0 else 7))
            r = rows_of(o) if t < 3 else half_rows(o, way)
            ref = W.at[c, 2, r, :]
            copy = special[way, t] = remote(ref, ref, at(dz=1 if way == 0 else 7))
            pl.when(third(o))(copy.start)

    def extra_side(o, rows=None):
        ref = W.at[c, 2, rows_of(o) if rows is None else rows, :]
        copy = remote(ref, ref, at(dc=1))
        special_side.append((o, copy))
        pl.when(third(o))(copy.start)

    def arrive(t):
        for way, sign in ((0, 1), (1, -1)):
            o = z - sign * (t + 1)
            for h in range(2) if t < 3 else (way,):
                ring[way, t, h].wait_recv()
            pl.when(third(o))(special[way, t].wait_recv)

    def pass_on(t):
        for way, sign in ((0, 1), (1, -1)):
            o = z - sign * (t + 1)
            for h in range(2) if t < 3 else (way,):
                share(h, o)
            extra_side(o, None if t < 3 else half_rows(o, way))

    launch(0)
    for h in range(2):
        share(h, z)
    extra_side(z)

    top_y.forward()
    low_x.forward()
    for d in (3, 1):
        top_more(d)
        low_more(d)
    top_x[0].forward()
    low_y[0].forward()
    top_y.finish()
    low_x.finish()
    top_more(2)
    low_more(2)
    arrive(0)
    launch(1)
    pass_on(0)
    for k in (1, 2):
        top_x[k].forward()
        low_y[k].forward()
    arrive(1)
    launch(2)
    pass_on(1)
    top_x[3].forward()
    low_y[3].forward()
    arrive(2)
    launch(3)
    pass_on(2)
    for k in range(4):
        top_x[k].finish()
        low_y[k].finish()
    for copy in metas:
        copy.wait_recv()
    for copy in local[2:]:
        copy.wait()
    arrive(3)
    pass_on(3)
    for copy in side:
        copy.wait_recv()
    for o, copy in special_side:
        pl.when(third(o))(copy.wait_recv)

    def multiply(k, unused):
        at_cols = pl.ds(pl.multiple_of(k * PART, 128), PART)
        lhs = T[:, :, at_cols].reshape(4 * BLOCK, PART)
        rhs = jnp.concatenate([W[m, h, at_cols, :] for m in range(2) for h in range(2)], axis=1)
        acc[...] += jnp.dot(lhs, rhs, preferred_element_type=jnp.float32)
        return unused

    acc[...] = jnp.zeros_like(acc)
    lax.fori_loop(0, 4, multiply, 0)
    lhs = T[:, :, cols(y)].reshape(4 * BLOCK, PART)
    rhs = jnp.concatenate([W[m, 2, cols(y), :] for m in range(2)], axis=1)
    last = jnp.dot(lhs, rhs, preferred_element_type=jnp.float32)
    for j in range(4):
        generated = mb[j * 2 + c, 1:2, :] == 1.0
        r = slice(j * BLOCK, (j + 1) * BLOCK)
        for h in range(2):
            ob[j, :, h * D : (h + 1) * D] = jnp.where(
                generated, acc[r, (2 + h) * D : (3 + h) * D], acc[r, h * D : (h + 1) * D]
            ).astype(jnp.bfloat16)
        vb[j] = jnp.where(generated, last[r, D:], last[r, :D])
    out = []
    for d in (1, 3, 2):
        there = (y + d) % 4
        out.append(go(vb.at[there], vp.at[y], at(dy=d)))
        out.append(go(ob.at[there], proj.at[y], at(dy=d)))
    proj[y] = ob[y]
    vp[y] = vb[y]
    for copy in out:
        copy.wait_recv()

    here = y * 2 + c
    kv[4, here, :BLOCK, :D] = proj[3, :, D:]
    kv[4, here, :BLOCK, D:] = (vp[0] + vp[1] + vp[2] + vp[3]).astype(jnp.bfloat16)
    kv[4, here, BLOCK:, :D] = jnp.broadcast_to(meta[0:1, :], (ROWS - BLOCK, D)).astype(jnp.bfloat16)
    kv[4, here, BLOCK:, D:] = jnp.zeros((ROWS - BLOCK, D), jnp.bfloat16)

    def kv_piece(p, j, half):
        r = pl.ds(0, ROWS) if half is None else (pl.ds(0, 64), pl.ds(64, ROWS - 64))[half]
        return kv.at[p, (j % 4) * 2 + c, r, :]

    def to_side(p, j):
        ref = kv_piece(p, j, None)
        out.append(go(ref, ref, at(dc=1)))
        return out[-1]

    back, around, crossed = [], [], []
    for t in range(5):
        p = 4 - t
        if t:
            back[-1].wait_recv()
        if t < 4:
            back.append(go(kv.at[p, here], kv.at[p - 1, here], at(dz=1)))
        around.append(Ring("dy", lambda j, h, p=p: kv_piece(p, j, h)))
        crossed.append(to_side(p, y))
        if t:
            around[t - 1].forward()
            crossed += [to_side(p + 1, y + 3), to_side(p + 1, y + 1)]
    around[4].forward()
    crossed += [to_side(0, y + 3), to_side(0, y + 1)]
    for t in range(5):
        around[t].finish()
        crossed.append(to_side(4 - t, y + 2))
    for copy in crossed:
        copy.wait_recv()

    conditional = {id(copy) for _, copy in ninth} | {id(copy) for copy in special.values()}
    conditional |= {id(copy) for _, copy in special_side}
    for copy in made:
        if id(copy) not in conditional:
            copy.wait_send()
    for d, copy in ninth:
        pl.when((y + d) % 4 == spread)(copy.wait_send)
    for (way, t), copy in special.items():
        pl.when(third(z - t if way == 0 else z + t))(copy.wait_send)
    for o, copy in special_side:
        pl.when(third(o))(copy.wait_send)


def gather_and_project(tokens, weights, meta):
    vmem = pl.BlockSpec(memory_space=pltpu.VMEM)
    return pl.pallas_call(
        project,
        name="project",
        out_shape=(
            jax.ShapeDtypeStruct((4, BLOCK, 2 * D), jnp.bfloat16),
            jax.ShapeDtypeStruct((5, 8, ROWS, 2 * D), jnp.bfloat16),
        ),
        in_specs=[vmem] * 3,
        out_specs=(vmem, vmem),
        scratch_shapes=[
            pltpu.VMEM((4, BLOCK, DEPTH), jnp.bfloat16),
            pltpu.VMEM((2, 3, DEPTH, D), jnp.bfloat16),
            pltpu.VMEM((8, 8, D), jnp.float32),
            pltpu.VMEM((4 * BLOCK, 4 * D), jnp.float32),
            pltpu.VMEM((4, BLOCK, 2 * D), jnp.bfloat16),
            pltpu.VMEM((4, BLOCK, D), jnp.float32),
            pltpu.VMEM((4, BLOCK, D), jnp.float32),
            pltpu.SemaphoreType.DMA((COPIES,)),
            pltpu.SemaphoreType.DMA((COPIES,)),
            pltpu.SemaphoreType.DMA((5,)),
        ],
        compiler_params=pltpu.CompilerParams(
            collective_id=0, has_side_effects=True, vmem_limit_bytes=40 << 20
        ),
    )(tokens, weights, meta)


def attend(place, proj, kv, o_ref, qa, ka, va, acc, top, seg):
    eye = (
        lax.broadcasted_iota(jnp.int32, (BLOCK, D), 0)
        == lax.broadcasted_iota(jnp.int32, (BLOCK, D), 1)
    ).astype(jnp.bfloat16)
    for h in range(HEADS):
        qa[h * BLOCK : (h + 1) * BLOCK, :D] = proj[h // 2, :, (h % 2) * D : (h % 2 + 1) * D]
        qa[h * BLOCK : (h + 1) * BLOCK, D:] = eye
    va[:, D:] = jnp.ones((WINDOW * BLOCK, D), jnp.bfloat16)
    first = place[1]
    missing = 32 - place[2]
    for j in range(WINDOW):
        row = kv[first + j, BLOCK:, :D][0:1].astype(jnp.float32)
        seg[j : j + 1, :] = jnp.where(j < missing, -1.0, row)
    seg_row = seg[WINDOW - 1 : WINDOW, :]
    seg_cols = seg[...].T
    key = lax.broadcasted_iota(jnp.int32, (BLOCK, BLOCK), 0)
    query = lax.broadcasted_iota(jnp.int32, (BLOCK, BLOCK), 1)
    reach = jnp.where(place[0] == 1, BLOCK, query)
    for j in range(WINDOW):
        rows = slice(j * BLOCK, (j + 1) * BLOCK)
        ka[rows, :D] = kv[first + j, :BLOCK, :D]
        va[rows, :D] = kv[first + j, :BLOCK, D:]
        same = seg_cols[:, j : j + 1] == seg_row
        if j == WINDOW - 1:
            same = same & (key <= reach)
        ka[rows, D:] = jnp.where(same, 0.0, FAR).astype(jnp.bfloat16)

    top[...] = jnp.full_like(top, -3e38)
    acc[...] = jnp.zeros_like(acc)

    def step(i, unused):
        c = CHUNKS - 1 - i
        rows = pl.ds(pl.multiple_of(c * (PER * BLOCK), BLOCK), PER * BLOCK)
        s = lax.dot_general(
            qa[...], ka[rows, :], (((1,), (1,)), ((), ())), preferred_element_type=jnp.float32
        )
        old = top[...]
        new = jnp.maximum(old, jnp.max(s, axis=1, keepdims=True))
        top[...] = new
        p = jnp.exp2((s - new) * SCALE).astype(jnp.bfloat16)
        shrink = jnp.exp2((old - new) * SCALE)
        acc[...] = acc[...] * shrink + jnp.dot(p, va[rows, :], preferred_element_type=jnp.float32)
        return unused

    lax.fori_loop(0, CHUNKS, step, 0)
    for h in range(HEADS):
        part = acc[h * BLOCK : (h + 1) * BLOCK, :]
        o_ref[:, h * D : (h + 1) * D] = (part[:, :D] / part[:, D:]).astype(jnp.bfloat16)


def attention(place, proj, kv):
    vmem = pl.BlockSpec(memory_space=pltpu.VMEM)
    return pl.pallas_call(
        attend,
        name="attend",
        out_shape=jax.ShapeDtypeStruct((BLOCK, HEADS * D), jnp.bfloat16),
        in_specs=[pl.BlockSpec(memory_space=pltpu.SMEM), vmem, vmem],
        out_specs=vmem,
        scratch_shapes=[
            pltpu.VMEM((HEADS * BLOCK, 2 * D), jnp.bfloat16),
            pltpu.VMEM((WINDOW * BLOCK, 2 * D), jnp.bfloat16),
            pltpu.VMEM((WINDOW * BLOCK, 2 * D), jnp.bfloat16),
            pltpu.VMEM((HEADS * BLOCK, 2 * D), jnp.float32),
            pltpu.VMEM((HEADS * BLOCK, 1), jnp.float32),
            pltpu.VMEM((40, BLOCK), jnp.float32),
        ],
        compiler_params=pltpu.CompilerParams(vmem_limit_bytes=48 << 20),
    )(place, proj, kv.reshape(40, ROWS, 2 * D))


def local(tokens, modality, segment, w_proj):
    here = lax.axis_index("seq")
    meta = jnp.concatenate(
        [
            segment.astype(jnp.float32)[None],
            jnp.broadcast_to(modality.astype(jnp.float32)[:, None], (1, BLOCK)),
            jnp.zeros((6, BLOCK), jnp.float32),
        ]
    )
    proj, kv = gather_and_project(tokens, w_proj, meta)
    place = jnp.stack([modality[0], here % 8, here])
    return attention(place, proj, kv)


def solution(mesh):
    return jax.shard_map(
        local,
        mesh=mesh,
        in_specs=(P("seq", "tp"), P("seq"), P("seq"), P(None, "seq", "tp")),
        out_specs=P("seq", "tp"),
        check_vma=False,
    )
```
